256 devices in a mesh: tm: 8 (over x, y_lo), pts: 32 (over y_hi, z, core).
Axes of the slice: x: 4, y: 4 (y_hi: 2, y_lo: 2; y = y_hi * 2 + y_lo), z: 8, core: 2. Of those that a mesh axis runs over, the one named last changes fastest.
Arguments:
- orbitals: bfloat16 [32768, 2048], P('pts'), may hold values from -6 to 6
- panel_orbitals: bfloat16 [1024, 2048], P(('tm', 'pts')), may hold values from -0.1796875 to 0.1796875
- band_gap: float32 [2048], replicated, may hold values from 0.1 to 1
- tau_points: float32 [8], replicated, may hold values from 0.1 to 2
- quad_weight: float32 [8], replicated, may hold values from 0.1 to 1
- frequencies: float32 [8], replicated, may hold values from 0.1 to 3
- coulomb: bfloat16 [1024, 1024], P(('tm', 'pts')), may hold values from -0.1875 to 0.1875
Outputs:
- screened: bfloat16 [8, 32768, 1024], P(None, ('pts', 'tm'))
The draws below stay inside these ranges and needn't reach their ends.
All inputs are finite; a program needn't handle non-finite values.
Results may differ from the reference program's by a relative error of at most 0.0056.
Values may be sent and summed in bfloat16 or wider, within the bound.
No kernel may reach another device: no remote copies, remote signals or barrier semaphores. Data moves between devices by JAX's collectives and lax.ppermute only.
A program may use at most 64 MiB of HBM per device.

```python
import math
import jax
import jax.numpy as jnp
from jax import lax

NOCC = 512
BANDS = 2048
PANEL = 1024
FREQS = 8
TAUS = 8
NPTS = 32768


def block_scale(key, dims, split, smallest, high):
    gain = 1.0
    for position, parts in split:
        draws = jax.random.uniform(jax.random.fold_in(jax.random.fold_in(key, 6), position), (parts,), jnp.float32, smallest / len(split), high / len(split))
        gain = gain * jnp.repeat(jnp.exp(draws), dims[position] // parts).reshape((-1,) + (1,) * (len(dims) - 1 - position))
    return gain


def gaussian(stream_key, shape, deviation, bound, split=(), dtype=jnp.bfloat16):
    result = jax.random.normal(stream_key, shape, jnp.float32) * deviation
    if len(split) > 0:
        result = block_scale(stream_key, shape, split, -0.22, 0.18) * result
    return jnp.clip(result, min=-bound, max=bound).astype(dtype)


def setup_inputs(seed: int = 0) -> dict:
    seeds = jax.random.split(jax.random.key(seed), 8)
    return {
        "orbitals": gaussian(seeds[0], (NPTS, BANDS), 1.0, 6.0, ((0, 32),)),
        "panel_orbitals": gaussian(seeds[1], (PANEL, BANDS), 0.03, 0.1796875, ((0, 256),)),
        "band_gap": jnp.clip(jnp.exp(jax.random.uniform(seeds[2], (BANDS,), jnp.float32, math.log(0.1), math.log(1.0))), 0.1, 1.0),
        "tau_points": jnp.clip(jnp.exp(jax.random.uniform(seeds[3], (TAUS,), jnp.float32, math.log(0.1), math.log(2.0))), 0.1, 2.0),
        "quad_weight": jnp.clip(jnp.exp(jax.random.uniform(seeds[4], (TAUS,), jnp.float32, math.log(0.1), math.log(1.0))), 0.1, 1.0),
        "frequencies": jnp.clip(jnp.exp(jax.random.uniform(seeds[5], (FREQS,), jnp.float32, math.log(0.1), math.log(3.0))), 0.1, 3.0),
        "coulomb": gaussian(seeds[6], (PANEL, PANEL), PANEL ** -0.5, 0.1875, ((0, 256),)),
    }


def contract(left, right):
    return lax.dot_general(left, right, (((1,), (1,)), ((), ())), preferred_element_type=jnp.float32)


def reference(orbitals, panel_orbitals, band_gap, tau_points, quad_weight, frequencies, coulomb):
    cosines = quad_weight[None, :] * jnp.cos(frequencies[:, None] * tau_points[None, :])
    occ_rows = orbitals[:, :NOCC]
    vir_rows = orbitals[:, NOCC:]
    layers = []
    for slot in range(TAUS):
        decay = jnp.exp(-band_gap * tau_points[slot])
        scaled = (panel_orbitals.astype(jnp.float32) * decay[None, :]).astype(jnp.bfloat16)
        green_occ = contract(occ_rows, scaled[:, :NOCC])
        green_vir = contract(vir_rows, scaled[:, NOCC:])
        layers.append((-(green_occ * green_vir)).astype(jnp.bfloat16))
    polar = jnp.stack(layers)
    flat = polar.reshape(TAUS, NPTS * PANEL).astype(jnp.float32)
    transformed = jnp.dot(cosines, flat, precision=lax.Precision.HIGHEST).astype(jnp.bfloat16)
    transformed = transformed.reshape(FREQS * NPTS, PANEL)
    screened = jnp.dot(transformed, coulomb, preferred_element_type=jnp.float32).astype(jnp.bfloat16)
    return screened.reshape(FREQS, NPTS, PANEL)
```

```python
import jax
import jax.numpy as jnp
from jax import lax
from jax.experimental import pallas as pl
from jax.experimental.pallas import tpu as pltpu
from jax.sharding import Mesh
from jax.sharding import PartitionSpec as P

NOCC = 512
BANDS = 2048
PANEL = 1024
FREQS = 8
TAUS = 8
COLS = 256

TM = ("x", "ylo")
PTS = ("yhi", "z", "core")
SIZES = (4, 2, 2, 8, 2)
Y = ("ylo", "yhi")


def along(value, axis, partner):
    size = lax.axis_size(axis)
    return lax.ppermute(value, axis, [(k, partner(k, size)) for k in range(size)])


def shifted(step):
    return lambda k, size: (k + step) % size


def shifted_y(step):
    def partner(k, size):
        y = (2 * (k % 2) + k // 2 + step) % size
        return 2 * (y % 2) + y // 2

    return partner


def flipped(bit):
    return lambda k, size: k ^ bit


def contract(left, right):
    return lax.dot_general(
        left, right, (((1,), (1,)), ((), ())), preferred_element_type=jnp.float32
    )


def screen_kernel(cosines_ref, scaled_ref, *refs):
    pieces, out_ref, transformed_ref = refs[:-2], refs[-2], refs[-1]
    height = pieces[0].shape[0]
    rows = scaled_ref.shape[0] // TAUS
    group = COLS // height
    for chunk in range(PANEL // COLS):
        held = pieces[chunk * group : (chunk + 1) * group]
        occ = jnp.concatenate([p[:, :NOCC] for p in held], axis=0)
        vir = jnp.concatenate([p[:, NOCC:BANDS] for p in held], axis=0)
        polar = -(contract(scaled_ref[:, :NOCC], occ) * contract(scaled_ref[:, NOCC:], vir))
        for k in range(FREQS):
            total = cosines_ref[k, 0] * polar[:rows]
            for t in range(1, TAUS):
                total += cosines_ref[k, t] * polar[t * rows : (t + 1) * rows]
            transformed_ref[k * rows : (k + 1) * rows, chunk * COLS : (chunk + 1) * COLS] = (
                total.astype(jnp.bfloat16)
            )
    for chunk in range(PANEL // COLS):
        start = BANDS + chunk * COLS
        coulomb = jnp.concatenate([p[:, start : start + COLS] for p in pieces], axis=0)
        out_ref[:, chunk * COLS : (chunk + 1) * COLS] = jnp.dot(
            transformed_ref[...], coulomb, preferred_element_type=jnp.float32
        ).astype(jnp.bfloat16)


def screen(cosines, scaled, pieces):
    rows = scaled.shape[0]
    vmem = pl.BlockSpec(memory_space=pltpu.VMEM)
    return pl.pallas_call(
        screen_kernel,
        out_shape=jax.ShapeDtypeStruct((rows, PANEL), jnp.bfloat16),
        in_specs=[pl.BlockSpec(memory_space=pltpu.SMEM), vmem] + [vmem] * len(pieces),
        out_specs=vmem,
        scratch_shapes=[pltpu.VMEM((rows, PANEL), jnp.bfloat16)],
        compiler_params=pltpu.CompilerParams(vmem_limit_bytes=40 * 2**20),
        cost_estimate=pl.CostEstimate(
            flops=2 * rows * PANEL * (BANDS + PANEL), bytes_accessed=2**24, transcendentals=0
        ),
    )(cosines, scaled, *pieces)


def shards(orbitals, panel_orbitals, band_gap, tau_points, quad_weight, frequencies, coulomb):
    held = jnp.concatenate([panel_orbitals, coulomb], axis=1)
    for bit in (4, 2, 1):
        held = jnp.concatenate([held, along(held, "z", flipped(bit))], axis=0)
    half = held.shape[0] // 2
    first, second = held[:half], held[half:]
    first = jnp.concatenate([first] + [along(first, Y, shifted_y(s)) for s in (1, 3, 2)], axis=0)
    second = jnp.concatenate([second] + [along(second, "x", shifted(s)) for s in (1, 3, 2)], axis=0)
    pieces = [first, second]
    for s in (1, 3, 2):
        pieces.append(along(first, "x", shifted(s)))
        pieces.append(along(second, Y, shifted_y(s)))
    pieces += [along(p, "core", flipped(1)) for p in pieces]

    rows = orbitals.shape[0] // lax.axis_size(TM)
    own = lax.dynamic_slice_in_dim(orbitals, lax.axis_index(TM) * rows, rows).astype(jnp.float32)
    decay = jnp.exp(-band_gap[None, :] * tau_points[:, None])
    scaled = (own[None] * decay[:, None, :]).astype(jnp.bfloat16).reshape(TAUS * rows, BANDS)
    cosines = quad_weight[None, :] * jnp.cos(frequencies[:, None] * tau_points[None, :])
    return screen(cosines, scaled, pieces).reshape(FREQS, rows, PANEL)


def solution(mesh):
    split = Mesh(mesh.devices.reshape(SIZES), TM + PTS)
    everywhere = P(TM + PTS, None)
    placed = (P(PTS, None), everywhere, P(), P(), P(), P(), everywhere)
    return jax.shard_map(
        shards, mesh=split, in_specs=placed, out_specs=P(None, PTS + TM, None), check_vma=False
    )
```

```python
import itertools

import jax
import jax.numpy as jnp
import numpy as np
from jax import lax
from jax.experimental import pallas as pl
from jax.experimental.pallas import tpu as pltpu
from jax.sharding import Mesh
from jax.sharding import PartitionSpec as P

NOCC = 512
BANDS = 2048
PANEL = 1024
FREQS = 8
TAUS = 8
COLS = 256

TM = ("x", "ylo")
PTS = ("yhi", "z", "core")
SIZES = (4, 2, 2, 8, 2)
RING = 4


def moved(value, target):
    pairs = []
    for source, (x, ylo, yhi, z, core) in enumerate(itertools.product(*map(range, SIZES))):
        x, y, z, core = target(x, 2 * yhi + ylo, z, core)
        place = (x % RING, y % 2, y % RING // 2, z % SIZES[3], core)
        pairs.append((source, int(np.ravel_multi_index(place, SIZES))))
    return lax.ppermute(value, TM + PTS, pairs)


def z_flip(bit):
    return lambda x, y, z, core: (x, y, z ^ bit, core)


def y_then_x(step):
    return lambda x, y, z, core: (x + step * core, y + step * (1 - core), z, core)


def x_then_y(step):
    return lambda x, y, z, core: (x + step * (1 - core), y + step * core, z, core)


def other_core(x, y, z, core):
    return x, y, z, 1 - core


def contract(left, right):
    return lax.dot_general(
        left, right, (((1,), (1,)), ((), ())), preferred_element_type=jnp.float32
    )


def transform_kernel(cosines_ref, scaled_ref, *refs):
    pieces, out_ref = refs[:-1], refs[-1]
    rows = scaled_ref.shape[0] // TAUS
    occ = jnp.concatenate([p[:, :NOCC] for p in pieces], axis=0)
    vir = jnp.concatenate([p[:, NOCC:BANDS] for p in pieces], axis=0)
    polar = -(contract(scaled_ref[:, :NOCC], occ) * contract(scaled_ref[:, NOCC:], vir))
    for k in range(FREQS):
        total = cosines_ref[k, 0] * polar[:rows]
        for t in range(1, TAUS):
            total += cosines_ref[k, t] * polar[t * rows : (t + 1) * rows]
        out_ref[k * rows : (k + 1) * rows, :] = total.astype(jnp.bfloat16)


def screen_kernel(*refs):
    blocks, pieces, out_ref = refs[:4], refs[4:-1], refs[-1]
    transformed = jnp.concatenate([b[...] for b in blocks], axis=1)
    for start in range(0, PANEL, COLS):
        columns = slice(BANDS + start, BANDS + start + COLS)
        coulomb = jnp.concatenate([p[:, columns] for p in pieces], axis=0)
        out_ref[:, start : start + COLS] = jnp.dot(
            transformed, coulomb, preferred_element_type=jnp.float32
        ).astype(jnp.bfloat16)


VMEM = pl.BlockSpec(memory_space=pltpu.VMEM)


def transform(cosines, scaled, pieces):
    rows, width = scaled.shape[0], sum(p.shape[0] for p in pieces)
    return pl.pallas_call(
        transform_kernel,
        out_shape=jax.ShapeDtypeStruct((rows, width), jnp.bfloat16),
        in_specs=[pl.BlockSpec(memory_space=pltpu.SMEM), VMEM] + [VMEM] * len(pieces),
        out_specs=VMEM,
        compiler_params=pltpu.CompilerParams(vmem_limit_bytes=24 * 2**20),
        cost_estimate=pl.CostEstimate(
            flops=2 * rows * width * BANDS, bytes_accessed=2**20, transcendentals=0
        ),
    )(cosines, scaled, *pieces)


def screen(blocks, pieces):
    rows = blocks[0].shape[0]
    return pl.pallas_call(
        screen_kernel,
        out_shape=jax.ShapeDtypeStruct((rows, PANEL), jnp.bfloat16),
        in_specs=[VMEM] * (len(blocks) + len(pieces)),
        out_specs=VMEM,
        compiler_params=pltpu.CompilerParams(vmem_limit_bytes=24 * 2**20),
        cost_estimate=pl.CostEstimate(
            flops=2 * rows * PANEL * PANEL, bytes_accessed=2**22, transcendentals=0
        ),
    )(*blocks, *pieces)


def join_kernel(*refs):
    del refs


def joined(values, after):
    return pl.pallas_call(
        join_kernel,
        out_shape=[jax.ShapeDtypeStruct(v.shape, v.dtype) for v in values],
        in_specs=[pl.BlockSpec(memory_space=pl.ANY)] * (len(values) + 1),
        out_specs=[pl.BlockSpec(memory_space=pl.ANY)] * len(values),
        input_output_aliases={k: k for k in range(len(values))},
        compiler_params=pltpu.CompilerParams(vmem_limit_bytes=2**20),
    )(*values, after)


def shards(orbitals, panel_orbitals, band_gap, tau_points, quad_weight, frequencies, coulomb):
    held = jnp.concatenate([panel_orbitals, coulomb], axis=1)
    for bit in (4, 2, 1):
        held = jnp.concatenate([held, moved(held, z_flip(bit))], axis=0)
    rows = orbitals.shape[0] // lax.axis_size(TM)
    own = lax.dynamic_slice_in_dim(orbitals, lax.axis_index(TM) * rows, rows).astype(jnp.float32)
    decay = jnp.exp(-band_gap[None, :] * tau_points[:, None])
    scaled = (own[None] * decay[:, None, :]).astype(jnp.bfloat16).reshape(TAUS * rows, BANDS)
    cosines = quad_weight[None, :] * jnp.cos(frequencies[:, None] * tau_points[None, :])

    held, cosines, scaled = lax.optimization_barrier((held, cosines, scaled))
    held = jnp.concatenate([held] + [moved(held, y_then_x(s)) for s in (1, 3, 2)], axis=0)
    others = [moved(held, x_then_y(s)) for s in (1, 3, 2)]
    both = [held, moved(held, other_core)]
    blocks, pieces = [transform(cosines, scaled, both)], both
    for chunk in joined(others, blocks[0]):
        both = [chunk, moved(chunk, other_core)]
        blocks.append(transform(cosines, scaled, both))
        pieces += both
    return screen(blocks, pieces).reshape(FREQS, rows, PANEL)


def solution(mesh):
    split = Mesh(mesh.devices.reshape(SIZES), TM + PTS)
    everywhere = P(TM + PTS, None)
    placed = (P(PTS, None), everywhere, P(), P(), P(), P(), everywhere)
    return jax.shard_map(
        shards, mesh=split, in_specs=placed, out_specs=P(None, PTS + TM, None), check_vma=False
    )
```

```python
import functools
import itertools

import jax
import jax.numpy as jnp
import numpy as np
from jax import lax
from jax.experimental import pallas as pl
from jax.experimental.pallas import tpu as pltpu
from jax.sharding import Mesh
from jax.sharding import PartitionSpec as P

NOCC = 512
BANDS = 2048
PANEL = 1024
FREQS = 8
TAUS = 8
COLS = 256

TM = ("x", "ylo")
PTS = ("yhi", "z", "core")
SIZES = (4, 2, 2, 8, 2)
RING = 4


def moved(value, target):
    pairs = []
    for source, (x, ylo, yhi, z, core) in enumerate(itertools.product(*map(range, SIZES))):
        x, y, z, core = target(x, 2 * yhi + ylo, z, core)
        place = (x % RING, y % 2, y % RING // 2, z % SIZES[3], core)
        pairs.append((source, int(np.ravel_multi_index(place, SIZES))))
    return lax.ppermute(value, TM + PTS, pairs)


def z_flip(bit):
    return lambda x, y, z, core: (x, y, z ^ bit, core)


def y_then_x(step):
    return lambda x, y, z, core: (x + step * core, y + step * (1 - core), z, core)


def x_then_y(step):
    return lambda x, y, z, core: (x + step * (1 - core), y + step * core, z, core)


def other_core(x, y, z, core):
    return x, y, z, 1 - core


def contract(left, right):
    return lax.dot_general(
        left, right, (((1,), (1,)), ((), ())), preferred_element_type=jnp.float32
    )


def polar_of(scaled_ref, pieces):
    occ = jnp.concatenate([p[:, :NOCC] for p in pieces], axis=0)
    vir = jnp.concatenate([p[:, NOCC:BANDS] for p in pieces], axis=0)
    return contract(scaled_ref[:, :NOCC], occ) * contract(scaled_ref[:, NOCC:], vir)


def at_frequency(weights_ref, polar, k):
    rows = polar.shape[0] // TAUS
    terms = [
        weights_ref[k * TAUS + t, :][None, :] * polar[t * rows : (t + 1) * rows] for t in range(TAUS)
    ]
    total = functools.reduce(jnp.add, terms)
    return total.astype(jnp.bfloat16)


def transform_kernel(weights_ref, scaled_ref, *refs):
    pieces, out_ref = refs[:-1], refs[-1]
    rows = scaled_ref.shape[0] // TAUS
    polar = polar_of(scaled_ref, pieces)
    for k in range(FREQS):
        out_ref[k * rows : (k + 1) * rows, :] = at_frequency(weights_ref, polar, k)


def first_kernel(weights_ref, decay_ref, rows_ref, *refs):
    pieces, (out_ref, scaled_ref) = refs[:-2], refs[-2:]
    rows = rows_ref.shape[0]
    for t in range(TAUS):
        scaled_ref[t * rows : (t + 1) * rows, :] = (
            rows_ref[...].astype(jnp.float32) * decay_ref[t, :][None, :]
        ).astype(jnp.bfloat16)
    transform_kernel(weights_ref, scaled_ref, *pieces, out_ref)


def screen_kernel(blocks_held, last_held, weights_ref, scaled_ref, *refs):
    blocks, refs = refs[:blocks_held], refs[blocks_held:]
    pieces, (out_ref, done_ref, sems) = refs[:-3], refs[-3:]
    rows = scaled_ref.shape[0] // TAUS
    polar = polar_of(scaled_ref, pieces[-last_held:])
    coulomb = jnp.concatenate([p[:, BANDS:] for p in pieces], axis=0)
    copies = []
    for step in range(FREQS // 2):
        here = slice(2 * step * rows, 2 * (step + 1) * rows)
        last = [at_frequency(weights_ref, polar, k) for k in (2 * step, 2 * step + 1)]
        transformed = jnp.concatenate(
            [b[here, :] for b in blocks] + [jnp.concatenate(last, axis=0)], axis=1
        )
        done_ref[here, :] = jnp.dot(
            transformed, coulomb, preferred_element_type=jnp.float32
        ).astype(jnp.bfloat16)
        copies.append(
            pltpu.make_async_copy(done_ref.at[here, :], out_ref.at[here, :], sems.at[step])
        )
        copies[-1].start()
    for copy in copies:
        copy.wait()


VMEM = pl.BlockSpec(memory_space=pltpu.VMEM)


def transform(weights, scaled, pieces):
    rows, width = scaled.shape[0], sum(p.shape[0] for p in pieces)
    return pl.pallas_call(
        transform_kernel,
        out_shape=jax.ShapeDtypeStruct((rows, width), jnp.bfloat16),
        in_specs=[VMEM] * (2 + len(pieces)),
        out_specs=VMEM,
        compiler_params=pltpu.CompilerParams(vmem_limit_bytes=12 * 2**20),
        cost_estimate=pl.CostEstimate(
            flops=2 * rows * width * BANDS, bytes_accessed=2**20, transcendentals=0
        ),
    )(weights, scaled, *pieces)


def transform_first(weights, decay, own, pieces):
    rows, width = TAUS * own.shape[0], sum(p.shape[0] for p in pieces)
    return pl.pallas_call(
        first_kernel,
        out_shape=[
            jax.ShapeDtypeStruct((rows, width), jnp.bfloat16),
            jax.ShapeDtypeStruct((rows, BANDS), jnp.bfloat16),
        ],
        in_specs=[VMEM] * (3 + len(pieces)),
        out_specs=[VMEM, VMEM],
        compiler_params=pltpu.CompilerParams(vmem_limit_bytes=12 * 2**20),
        cost_estimate=pl.CostEstimate(
            flops=2 * rows * width * BANDS, bytes_accessed=2**20, transcendentals=0
        ),
    )(weights, decay, own, *pieces)


def screen(weights, scaled, blocks, pieces, last):
    rows = scaled.shape[0]
    pieces = pieces + last
    return pl.pallas_call(
        functools.partial(screen_kernel, len(blocks), len(last)),
        out_shape=jax.ShapeDtypeStruct((rows, PANEL), jnp.bfloat16),
        in_specs=[VMEM] * (2 + len(blocks) + len(pieces)),
        out_specs=pl.BlockSpec(memory_space=pl.ANY),
        scratch_shapes=[
            pltpu.VMEM((rows, PANEL), jnp.bfloat16),
            pltpu.SemaphoreType.DMA((FREQS // 2,)),
        ],
        compiler_params=pltpu.CompilerParams(vmem_limit_bytes=12 * 2**20),
        cost_estimate=pl.CostEstimate(
            flops=2 * rows * PANEL * (PANEL + BANDS // 4), bytes_accessed=2**22, transcendentals=0
        ),
    )(weights, scaled, *blocks, *pieces)


def join_kernel(*refs):
    del refs


def joined(values, after):
    return pl.pallas_call(
        join_kernel,
        out_shape=[jax.ShapeDtypeStruct(v.shape, v.dtype) for v in values],
        in_specs=[pl.BlockSpec(memory_space=pl.ANY)] * (len(values) + 1),
        out_specs=[pl.BlockSpec(memory_space=pl.ANY)] * len(values),
        input_output_aliases={k: k for k in range(len(values))},
        compiler_params=pltpu.CompilerParams(vmem_limit_bytes=2**20),
    )(*values, after)


def shards(orbitals, panel_orbitals, band_gap, tau_points, quad_weight, frequencies, coulomb):
    held = jnp.pad(panel_orbitals, ((0, 0), (0, PANEL))) + jnp.pad(coulomb, ((0, 0), (BANDS, 0)))
    for bit in (4, 2, 1):
        held = jnp.concatenate([held, moved(held, z_flip(bit))], axis=0)
    rows = orbitals.shape[0] // lax.axis_size(TM)
    own = lax.dynamic_slice_in_dim(orbitals, lax.axis_index(TM) * rows, rows)
    decay = jnp.exp(-band_gap[None, :] * tau_points[:, None])
    weights = -quad_weight[None, :] * jnp.cos(frequencies[:, None] * tau_points[None, :])
    weights = jnp.broadcast_to(weights.reshape(FREQS * TAUS, 1), (FREQS * TAUS, COLS))

    held, weights, decay, own = lax.optimization_barrier((held, weights, decay, own))
    held = jnp.concatenate([held] + [moved(held, y_then_x(s)) for s in (1, -1, 2)], axis=0)
    others = [moved(held, x_then_y(s)) for s in (1, -1, 2)]
    pieces = [held, moved(held, other_core)]
    block, scaled = transform_first(weights, decay, own, pieces)
    blocks = [block]
    below, above, far = joined(others, blocks[0])
    for chunk in (below, above):
        both = [chunk, moved(chunk, other_core)]
        blocks.append(transform(weights, scaled, both))
        pieces += both
    last = [far, moved(far, other_core)]
    return screen(weights, scaled, blocks, pieces, last).reshape(FREQS, rows, PANEL)


def solution(mesh):
    split = Mesh(mesh.devices.reshape(SIZES), TM + PTS)
    everywhere = P(TM + PTS, None)
    placed = (P(PTS, None), everywhere, P(), P(), P(), P(), everywhere)
    return jax.shard_map(
        shards, mesh=split, in_specs=placed, out_specs=P(None, PTS + TM, None), check_vma=False
    )
```

```python
import functools
import itertools

import jax
import jax.numpy as jnp
import numpy as np
from jax import lax
from jax.experimental import pallas as pl
from jax.experimental.pallas import tpu as pltpu
from jax.sharding import Mesh
from jax.sharding import PartitionSpec as P

NOCC = 512
BANDS = 2048
PANEL = 1024
FREQS = 8
TAUS = 8
COLS = 256

TM = ("x", "ylo")
PTS = ("yhi", "z", "core")
SIZES = (4, 2, 2, 8, 2)


def moved(value, target):
    pairs = []
    for source, (x, ylo, yhi, z, core) in enumerate(itertools.product(*map(range, SIZES))):
        x, y, z, core = target(x, 2 * yhi + ylo, z, core)
        place = (x, y % 2, y // 2, z, core)
        pairs.append((source, int(np.ravel_multi_index(place, SIZES))))
    return lax.ppermute(value, TM + PTS, pairs)


def z_flip(bit):
    return lambda x, y, z, core: (x, y, z ^ bit, core)


def y_then_x(bits):
    return lambda x, y, z, core: (x ^ bits * core, y ^ bits * (1 - core), z, core)


def x_then_y(bits):
    return lambda x, y, z, core: (x ^ bits * (1 - core), y ^ bits * core, z, core)


def other_core(x, y, z, core):
    return x, y, z, 1 - core


def contract(left, right):
    return lax.dot_general(
        left, right, (((1,), (1,)), ((), ())), preferred_element_type=jnp.float32
    )


def polar_of(scaled_ref, pieces):
    occ = jnp.concatenate([p[:, :NOCC] for p in pieces], axis=0)
    vir = jnp.concatenate([p[:, NOCC:BANDS] for p in pieces], axis=0)
    return contract(scaled_ref[:, :NOCC], occ) * contract(scaled_ref[:, NOCC:], vir)


def at_frequency(weights_ref, polar, k):
    rows = polar.shape[0] // TAUS
    terms = [
        weights_ref[k * TAUS + t, :][None, :] * polar[t * rows : (t + 1) * rows] for t in range(TAUS)
    ]
    total = functools.reduce(jnp.add, terms)
    return total.astype(jnp.bfloat16)


def transform_kernel(weights_ref, scaled_ref, *refs):
    pieces, out_ref = refs[:-1], refs[-1]
    rows = scaled_ref.shape[0] // TAUS
    polar = polar_of(scaled_ref, pieces)
    for k in range(FREQS):
        out_ref[k * rows : (k + 1) * rows, :] = at_frequency(weights_ref, polar, k)


def first_kernel(weights_ref, decay_ref, rows_ref, *refs):
    pieces, (out_ref, scaled_ref) = refs[:-2], refs[-2:]
    rows = rows_ref.shape[0]
    for t in range(TAUS):
        scaled_ref[t * rows : (t + 1) * rows, :] = (
            rows_ref[...].astype(jnp.float32) * decay_ref[t, :][None, :]
        ).astype(jnp.bfloat16)
    transform_kernel(weights_ref, scaled_ref, *pieces, out_ref)


def screen_kernel(blocks_held, last_held, weights_ref, scaled_ref, *refs):
    blocks, refs = refs[:blocks_held], refs[blocks_held:]
    pieces, (out_ref, done_ref, sems) = refs[:-3], refs[-3:]
    rows = scaled_ref.shape[0] // TAUS
    polar = polar_of(scaled_ref, pieces[-last_held:])
    coulomb = jnp.concatenate([p[:, BANDS:] for p in pieces], axis=0)
    copies = []
    for step in range(FREQS // 2):
        here = slice(2 * step * rows, 2 * (step + 1) * rows)
        last = [at_frequency(weights_ref, polar, k) for k in (2 * step, 2 * step + 1)]
        transformed = jnp.concatenate(
            [b[here, :] for b in blocks] + [jnp.concatenate(last, axis=0)], axis=1
        )
        done_ref[here, :] = jnp.dot(
            transformed, coulomb, preferred_element_type=jnp.float32
        ).astype(jnp.bfloat16)
        copies.append(
            pltpu.make_async_copy(done_ref.at[here, :], out_ref.at[here, :], sems.at[step])
        )
        copies[-1].start()
    for copy in copies:
        copy.wait()


VMEM = pl.BlockSpec(memory_space=pltpu.VMEM)


def transform(weights, scaled, pieces):
    rows, width = scaled.shape[0], sum(p.shape[0] for p in pieces)
    return pl.pallas_call(
        transform_kernel,
        out_shape=jax.ShapeDtypeStruct((rows, width), jnp.bfloat16),
        in_specs=[VMEM] * (2 + len(pieces)),
        out_specs=VMEM,
        compiler_params=pltpu.CompilerParams(vmem_limit_bytes=12 * 2**20),
        cost_estimate=pl.CostEstimate(
            flops=2 * rows * width * BANDS, bytes_accessed=2**20, transcendentals=0
        ),
    )(weights, scaled, *pieces)


def transform_first(weights, decay, own, pieces):
    rows, width = TAUS * own.shape[0], sum(p.shape[0] for p in pieces)
    return pl.pallas_call(
        first_kernel,
        out_shape=[
            jax.ShapeDtypeStruct((rows, width), jnp.bfloat16),
            jax.ShapeDtypeStruct((rows, BANDS), jnp.bfloat16),
        ],
        in_specs=[VMEM] * (3 + len(pieces)),
        out_specs=[VMEM, VMEM],
        compiler_params=pltpu.CompilerParams(vmem_limit_bytes=12 * 2**20),
        cost_estimate=pl.CostEstimate(
            flops=2 * rows * width * BANDS, bytes_accessed=2**20, transcendentals=0
        ),
    )(weights, decay, own, *pieces)


def screen(weights, scaled, blocks, pieces, last):
    rows = scaled.shape[0]
    pieces = pieces + last
    return pl.pallas_call(
        functools.partial(screen_kernel, len(blocks), len(last)),
        out_shape=jax.ShapeDtypeStruct((rows, PANEL), jnp.bfloat16),
        in_specs=[VMEM] * (2 + len(blocks) + len(pieces)),
        out_specs=pl.BlockSpec(memory_space=pl.ANY),
        scratch_shapes=[
            pltpu.VMEM((rows, PANEL), jnp.bfloat16),
            pltpu.SemaphoreType.DMA((FREQS // 2,)),
        ],
        compiler_params=pltpu.CompilerParams(vmem_limit_bytes=12 * 2**20),
        cost_estimate=pl.CostEstimate(
            flops=2 * rows * PANEL * (PANEL + BANDS // 4), bytes_accessed=2**22, transcendentals=0
        ),
    )(weights, scaled, *blocks, *pieces)


def shards(orbitals, panel_orbitals, band_gap, tau_points, quad_weight, frequencies, coulomb):
    held = jnp.pad(panel_orbitals, ((0, 0), (0, PANEL))) + jnp.pad(coulomb, ((0, 0), (BANDS, 0)))
    for bit in (4, 2, 1):
        held = jnp.concatenate([held, moved(held, z_flip(bit))], axis=0)
    rows = orbitals.shape[0] // lax.axis_size(TM)
    own = lax.dynamic_slice_in_dim(orbitals, lax.axis_index(TM) * rows, rows)
    decay = jnp.exp(-band_gap[None, :] * tau_points[:, None])
    weights = -quad_weight[None, :] * jnp.cos(frequencies[:, None] * tau_points[None, :])
    weights = jnp.broadcast_to(weights.reshape(FREQS * TAUS, 1), (FREQS * TAUS, COLS))

    held, weights, decay, own = lax.optimization_barrier((held, weights, decay, own))
    held = jnp.concatenate([held] + [moved(held, y_then_x(bits)) for bits in (1, 3, 2)], axis=0)
    half = held.shape[0] // 2
    near = [moved(held, x_then_y(bits)) for bits in (1, 3)]
    pieces = [held, moved(held, other_core)]
    block, scaled = transform_first(weights, decay, own, pieces)
    blocks = [block]
    near[0], near[1], blocks[0] = lax.optimization_barrier((near[0], near[1], blocks[0]))
    far = [moved(near[1][:half], x_then_y(1)), moved(near[0][half:], x_then_y(3))]
    for chunk in near:
        both = [chunk, moved(chunk, other_core)]
        blocks.append(transform(weights, scaled, both))
        pieces += both
    far[0], far[1], blocks[1], blocks[2] = lax.optimization_barrier((*far, *blocks[1:]))
    last = far + [moved(piece, other_core) for piece in far]
    return screen(weights, scaled, blocks, pieces, last).reshape(FREQS, rows, PANEL)


def solution(mesh):
    split = Mesh(mesh.devices.reshape(SIZES), TM + PTS)
    everywhere = P(TM + PTS, None)
    placed = (P(PTS, None), everywhere, P(), P(), P(), P(), everywhere)
    return jax.shard_map(
        shards, mesh=split, in_specs=placed, out_specs=P(None, PTS + TM, None), check_vma=False
    )
```

```python
import functools
import itertools

import jax
import jax.numpy as jnp
import numpy as np
from jax import lax
from jax.experimental import pallas as pl
from jax.experimental.pallas import tpu as pltpu
from jax.sharding import Mesh
from jax.sharding import PartitionSpec as P

NOCC = 512
BANDS = 2048
PANEL = 1024
FREQS = 8
TAUS = 8
COLS = 256
STEPS = 4

TM = ("x", "ylo")
PTS = ("yhi", "z", "core")
SIZES = (4, 2, 2, 8, 2)


def moved(value, target):
    pairs = []
    for source, (x, ylo, yhi, z, core) in enumerate(itertools.product(*map(range, SIZES))):
        x, y, z, core = target(x, 2 * yhi + ylo, z, core)
        place = (x, y % 2, y // 2, z, core)
        pairs.append((source, int(np.ravel_multi_index(place, SIZES))))
    return lax.ppermute(value, TM + PTS, pairs)


def z_flip(bit):
    return lambda x, y, z, core: (x, y, z ^ bit, core)


def y_then_x(bits):
    return lambda x, y, z, core: (x ^ bits * core, y ^ bits * (1 - core), z, core)


def x_then_y(bits):
    return lambda x, y, z, core: (x ^ bits * (1 - core), y ^ bits * core, z, core)


def other_core(x, y, z, core):
    return x, y, z, 1 - core


def contract(left, right):
    return lax.dot_general(
        left, right, (((1,), (1,)), ((), ())), preferred_element_type=jnp.float32
    )


def polar_of(scaled_ref, pieces):
    occ = jnp.concatenate([p[:, :NOCC] for p in pieces], axis=0)
    vir = jnp.concatenate([p[:, NOCC:BANDS] for p in pieces], axis=0)
    return contract(scaled_ref[:, :NOCC], occ) * contract(scaled_ref[:, NOCC:], vir)


def at_frequency(weights_ref, polar, k):
    rows = polar.shape[0] // TAUS
    terms = [
        weights_ref[k * TAUS + t, :][None, :] * polar[t * rows : (t + 1) * rows] for t in range(TAUS)
    ]
    total = functools.reduce(jnp.add, terms)
    return total.astype(jnp.bfloat16)


def transform_kernel(weights_ref, scaled_ref, *refs):
    pieces, out_ref = refs[:-1], refs[-1]
    rows = scaled_ref.shape[0] // TAUS
    polar = polar_of(scaled_ref, pieces)
    for k in range(FREQS):
        out_ref[k * rows : (k + 1) * rows, :] = at_frequency(weights_ref, polar, k)


def first_kernel(weights_ref, decay_ref, rows_ref, *refs):
    pieces, (out_ref, scaled_ref) = refs[:-2], refs[-2:]
    rows = rows_ref.shape[0]
    for t in range(TAUS):
        scaled_ref[t * rows : (t + 1) * rows, :] = (
            rows_ref[...].astype(jnp.float32) * decay_ref[t, :][None, :]
        ).astype(jnp.bfloat16)
    transform_kernel(weights_ref, scaled_ref, *pieces, out_ref)


def screen_kernel(*refs):
    pieces, out_ref = refs[:-1], refs[-1]
    held = len(pieces) // 3
    blocks, pieces = pieces[:held], pieces[held:]
    coulomb = jnp.concatenate([p[:, BANDS:] for p in pieces], axis=0)
    step = out_ref.shape[0] // STEPS
    for start in range(0, out_ref.shape[0], step):
        here = slice(start, start + step)
        transformed = jnp.concatenate([b[here, :] for b in blocks], axis=1)
        out_ref[here, :] = jnp.dot(transformed, coulomb, preferred_element_type=jnp.float32)


def last_kernel(weights_ref, scaled_ref, partial_ref, *refs):
    pieces, (out_ref, done_ref, sems) = refs[:-3], refs[-3:]
    rows = scaled_ref.shape[0] // TAUS
    polar = polar_of(scaled_ref, pieces)
    coulomb = jnp.concatenate([p[:, BANDS:] for p in pieces], axis=0)
    count = FREQS // STEPS
    copies = []
    for step in range(STEPS):
        here = slice(step * count * rows, (step + 1) * count * rows)
        some = range(step * count, (step + 1) * count)
        transformed = jnp.concatenate([at_frequency(weights_ref, polar, k) for k in some], axis=0)
        product = jnp.dot(transformed, coulomb, preferred_element_type=jnp.float32)
        done_ref[here, :] = (partial_ref[here, :] + product).astype(jnp.bfloat16)
        copies.append(
            pltpu.make_async_copy(done_ref.at[here, :], out_ref.at[here, :], sems.at[step])
        )
        copies[-1].start()
    for copy in copies:
        copy.wait()


VMEM = pl.BlockSpec(memory_space=pltpu.VMEM)


def transform(weights, scaled, pieces):
    rows, width = scaled.shape[0], sum(p.shape[0] for p in pieces)
    return pl.pallas_call(
        transform_kernel,
        out_shape=jax.ShapeDtypeStruct((rows, width), jnp.bfloat16),
        in_specs=[VMEM] * (2 + len(pieces)),
        out_specs=VMEM,
        compiler_params=pltpu.CompilerParams(vmem_limit_bytes=12 * 2**20),
        cost_estimate=pl.CostEstimate(
            flops=2 * rows * width * BANDS, bytes_accessed=2**20, transcendentals=0
        ),
    )(weights, scaled, *pieces)


def transform_first(weights, decay, own, pieces):
    rows, width = TAUS * own.shape[0], sum(p.shape[0] for p in pieces)
    return pl.pallas_call(
        first_kernel,
        out_shape=[
            jax.ShapeDtypeStruct((rows, width), jnp.bfloat16),
            jax.ShapeDtypeStruct((rows, BANDS), jnp.bfloat16),
        ],
        in_specs=[VMEM] * (3 + len(pieces)),
        out_specs=[VMEM, VMEM],
        compiler_params=pltpu.CompilerParams(vmem_limit_bytes=12 * 2**20),
        cost_estimate=pl.CostEstimate(
            flops=2 * rows * width * BANDS, bytes_accessed=2**20, transcendentals=0
        ),
    )(weights, decay, own, *pieces)


def screen(blocks, pieces):
    rows = blocks[0].shape[0]
    return pl.pallas_call(
        screen_kernel,
        out_shape=jax.ShapeDtypeStruct((rows, PANEL), jnp.float32),
        in_specs=[VMEM] * (len(blocks) + len(pieces)),
        out_specs=VMEM,
        compiler_params=pltpu.CompilerParams(vmem_limit_bytes=12 * 2**20),
        cost_estimate=pl.CostEstimate(
            flops=2 * rows * COLS * len(blocks) * PANEL, bytes_accessed=2**20, transcendentals=0
        ),
    )(*blocks, *pieces)


def screen_last(weights, scaled, partial, pieces):
    rows = scaled.shape[0]
    return pl.pallas_call(
        last_kernel,
        out_shape=jax.ShapeDtypeStruct((rows, PANEL), jnp.bfloat16),
        in_specs=[VMEM] * (3 + len(pieces)),
        out_specs=pl.BlockSpec(memory_space=pl.ANY),
        scratch_shapes=[
            pltpu.VMEM((rows, PANEL), jnp.bfloat16),
            pltpu.SemaphoreType.DMA((STEPS,)),
        ],
        compiler_params=pltpu.CompilerParams(vmem_limit_bytes=12 * 2**20),
        cost_estimate=pl.CostEstimate(
            flops=2 * rows * COLS * (PANEL + BANDS), bytes_accessed=2**22, transcendentals=0
        ),
    )(weights, scaled, partial, *pieces)


def shards(orbitals, panel_orbitals, band_gap, tau_points, quad_weight, frequencies, coulomb):
    held = jnp.pad(panel_orbitals, ((0, 0), (0, PANEL))) + jnp.pad(coulomb, ((0, 0), (BANDS, 0)))
    for bit in (4, 2, 1):
        held = jnp.concatenate([held, moved(held, z_flip(bit))], axis=0)
    rows = orbitals.shape[0] // lax.axis_size(TM)
    own = lax.dynamic_slice_in_dim(orbitals, lax.axis_index(TM) * rows, rows)
    decay = jnp.exp(-band_gap[None, :] * tau_points[:, None])
    weights = -quad_weight[None, :] * jnp.cos(frequencies[:, None] * tau_points[None, :])
    weights = jnp.broadcast_to(weights.reshape(FREQS * TAUS, 1), (FREQS * TAUS, COLS))

    held, weights, decay, own = lax.optimization_barrier((held, weights, decay, own))
    held = jnp.concatenate([held] + [moved(held, y_then_x(bits)) for bits in (2, 1, 3)], axis=0)
    half = held.shape[0] // 2
    near = [moved(held, x_then_y(bits)) for bits in (1, 3)]
    pieces = [held, moved(held, other_core)]
    block, scaled = transform_first(weights, decay, own, pieces)
    blocks = [block]
    near[0], near[1], blocks[0] = lax.optimization_barrier((near[0], near[1], blocks[0]))
    far = [moved(near[1][:half], x_then_y(1)), moved(near[0][half:], x_then_y(3))]
    for chunk in near:
        both = [chunk, moved(chunk, other_core)]
        blocks.append(transform(weights, scaled, both))
        pieces += both
    partial = screen(blocks, pieces)
    far[0], partial = lax.optimization_barrier((far[0], partial))
    far[1], partial = lax.optimization_barrier((far[1], partial))
    last = far + [moved(piece, other_core) for piece in far]
    return screen_last(weights, scaled, partial, last).reshape(FREQS, rows, PANEL)


def solution(mesh):
    split = Mesh(mesh.devices.reshape(SIZES), TM + PTS)
    everywhere = P(TM + PTS, None)
    placed = (P(PTS, None), everywhere, P(), P(), P(), P(), everywhere)
    return jax.shard_map(
        shards, mesh=split, in_specs=placed, out_specs=P(None, PTS + TM, None), check_vma=False
    )
```

```python
import functools
import itertools

import jax
import jax.numpy as jnp
import numpy as np
from jax import lax
from jax.experimental import pallas as pl
from jax.experimental.pallas import tpu as pltpu
from jax.sharding import Mesh
from jax.sharding import PartitionSpec as P

NOCC = 512
BANDS = 2048
PANEL = 1024
FREQS = 8
TAUS = 8
COLS = 256
STEPS = 4

TM = ("x", "ylo")
PTS = ("yhi", "z", "core")
SIZES = (4, 2, 2, 8, 2)


def moved(value, target):
    pairs = []
    for source, (x, ylo, yhi, z, core) in enumerate(itertools.product(*map(range, SIZES))):
        x, y, z, core = target(x, 2 * yhi + ylo, z, core)
        place = (x, y % 2, y // 2, z, core)
        pairs.append((source, int(np.ravel_multi_index(place, SIZES))))
    return lax.ppermute(value, TM + PTS, pairs)


def z_flip(bit):
    return lambda x, y, z, core: (x, y, z ^ bit, core)


def y_then_x(bits):
    return lambda x, y, z, core: (x ^ bits * core, y ^ bits * (1 - core), z, core)


def x_then_y(bits):
    return lambda x, y, z, core: (x ^ bits * (1 - core), y ^ bits * core, z, core)


def other_core(x, y, z, core):
    return x, y, z, 1 - core


def contract(left, right):
    return lax.dot_general(
        left, right, (((1,), (1,)), ((), ())), preferred_element_type=jnp.float32
    )


def polar_of(scaled_ref, pieces):
    occ = jnp.concatenate([p[:, :NOCC] for p in pieces], axis=0)
    vir = jnp.concatenate([p[:, NOCC:BANDS] for p in pieces], axis=0)
    return contract(scaled_ref[:, :NOCC], occ) * contract(scaled_ref[:, NOCC:], vir)


def at_frequency(weights_ref, polar, k):
    rows = polar.shape[0] // TAUS
    terms = [
        weights_ref[k * TAUS + t, :][None, :] * polar[t * rows : (t + 1) * rows] for t in range(TAUS)
    ]
    total = functools.reduce(jnp.add, terms)
    return total.astype(jnp.bfloat16)


def transform_kernel(weights_ref, scaled_ref, *refs):
    pieces, out_ref = refs[:-1], refs[-1]
    rows = scaled_ref.shape[0] // TAUS
    polar = polar_of(scaled_ref, pieces)
    for k in range(FREQS):
        out_ref[k * rows : (k + 1) * rows, :] = at_frequency(weights_ref, polar, k)


def first_kernel(weights_ref, decay_ref, rows_ref, *refs):
    pieces, (out_ref, scaled_ref) = refs[:-2], refs[-2:]
    rows = rows_ref.shape[0]
    for t in range(TAUS):
        scaled_ref[t * rows : (t + 1) * rows, :] = (
            rows_ref[...].astype(jnp.float32) * decay_ref[t, :][None, :]
        ).astype(jnp.bfloat16)
    transform_kernel(weights_ref, scaled_ref, *pieces, out_ref)


def screen_kernel(*refs):
    pieces, out_ref = refs[:-1], refs[-1]
    held = len(pieces) // 3
    blocks, pieces = pieces[:held], pieces[held:]
    coulomb = jnp.concatenate([p[:, BANDS:] for p in pieces], axis=0)
    step = out_ref.shape[0] // STEPS
    for start in range(0, out_ref.shape[0], step):
        here = slice(start, start + step)
        transformed = jnp.concatenate([b[here, :] for b in blocks], axis=1)
        out_ref[here, :] = jnp.dot(transformed, coulomb, preferred_element_type=jnp.float32)


def last_kernel(weights_ref, scaled_ref, partial_ref, *refs):
    pieces, (out_ref, done_ref, sems) = refs[:-3], refs[-3:]
    rows = scaled_ref.shape[0] // TAUS
    polar = polar_of(scaled_ref, pieces)
    coulomb = jnp.concatenate([p[:, BANDS:] for p in pieces], axis=0)
    count = FREQS // STEPS
    copies = []
    for step in range(STEPS):
        here = slice(step * count * rows, (step + 1) * count * rows)
        some = range(step * count, (step + 1) * count)
        transformed = jnp.concatenate([at_frequency(weights_ref, polar, k) for k in some], axis=0)
        product = jnp.dot(transformed, coulomb, preferred_element_type=jnp.float32)
        done_ref[here, :] = (partial_ref[here, :] + product).astype(jnp.bfloat16)
        copies.append(
            pltpu.make_async_copy(done_ref.at[here, :], out_ref.at[here, :], sems.at[step])
        )
        copies[-1].start()
    for copy in copies:
        copy.wait()


VMEM = pl.BlockSpec(memory_space=pltpu.VMEM)


def transform(weights, scaled, pieces):
    rows, width = scaled.shape[0], sum(p.shape[0] for p in pieces)
    return pl.pallas_call(
        transform_kernel,
        out_shape=jax.ShapeDtypeStruct((rows, width), jnp.bfloat16),
        in_specs=[VMEM] * (2 + len(pieces)),
        out_specs=VMEM,
        compiler_params=pltpu.CompilerParams(vmem_limit_bytes=12 * 2**20),
        cost_estimate=pl.CostEstimate(
            flops=2 * rows * width * BANDS, bytes_accessed=2**20, transcendentals=0
        ),
    )(weights, scaled, *pieces)


def transform_first(weights, decay, own, pieces):
    rows, width = TAUS * own.shape[0], sum(p.shape[0] for p in pieces)
    return pl.pallas_call(
        first_kernel,
        out_shape=[
            jax.ShapeDtypeStruct((rows, width), jnp.bfloat16),
            jax.ShapeDtypeStruct((rows, BANDS), jnp.bfloat16),
        ],
        in_specs=[VMEM] * (3 + len(pieces)),
        out_specs=[VMEM, VMEM],
        compiler_params=pltpu.CompilerParams(vmem_limit_bytes=12 * 2**20),
        cost_estimate=pl.CostEstimate(
            flops=2 * rows * width * BANDS, bytes_accessed=2**20, transcendentals=0
        ),
    )(weights, decay, own, *pieces)


def screen(blocks, pieces):
    rows = blocks[0].shape[0]
    return pl.pallas_call(
        screen_kernel,
        out_shape=jax.ShapeDtypeStruct((rows, PANEL), jnp.float32),
        in_specs=[VMEM] * (len(blocks) + len(pieces)),
        out_specs=VMEM,
        compiler_params=pltpu.CompilerParams(vmem_limit_bytes=12 * 2**20),
        cost_estimate=pl.CostEstimate(
            flops=2 * rows * COLS * len(blocks) * PANEL, bytes_accessed=2**20, transcendentals=0
        ),
    )(*blocks, *pieces)


def screen_last(weights, scaled, partial, pieces):
    rows = scaled.shape[0]
    return pl.pallas_call(
        last_kernel,
        out_shape=jax.ShapeDtypeStruct((rows, PANEL), jnp.bfloat16),
        in_specs=[VMEM] * (3 + len(pieces)),
        out_specs=pl.BlockSpec(memory_space=pl.ANY),
        scratch_shapes=[
            pltpu.VMEM((rows, PANEL), jnp.bfloat16),
            pltpu.SemaphoreType.DMA((STEPS,)),
        ],
        compiler_params=pltpu.CompilerParams(vmem_limit_bytes=12 * 2**20),
        cost_estimate=pl.CostEstimate(
            flops=2 * rows * COLS * (PANEL + BANDS), bytes_accessed=2**22, transcendentals=0
        ),
    )(weights, scaled, partial, *pieces)


def shards(orbitals, panel_orbitals, band_gap, tau_points, quad_weight, frequencies, coulomb):
    held = jnp.pad(panel_orbitals, ((0, 0), (0, PANEL))) + jnp.pad(coulomb, ((0, 0), (BANDS, 0)))
    for group in ((1,), (4, 6, 2)):
        held = jnp.concatenate([held] + [moved(held, z_flip(bits)) for bits in group], axis=0)
    rows = orbitals.shape[0] // lax.axis_size(TM)
    own = lax.dynamic_slice_in_dim(orbitals, lax.axis_index(TM) * rows, rows)
    decay = jnp.exp(-band_gap[None, :] * tau_points[:, None])
    weights = -quad_weight[None, :] * jnp.cos(frequencies[:, None] * tau_points[None, :])
    weights = jnp.broadcast_to(weights.reshape(FREQS * TAUS, 1), (FREQS * TAUS, COLS))

    held, weights, decay, own = lax.optimization_barrier((held, weights, decay, own))
    held = jnp.concatenate([held] + [moved(held, y_then_x(bits)) for bits in (2, 1, 3)], axis=0)
    half = held.shape[0] // 2
    near = [moved(held, x_then_y(bits)) for bits in (1, 3)]
    pieces = [held, moved(held, other_core)]
    block, scaled = transform_first(weights, decay, own, pieces)
    blocks = [block]
    near[0], near[1], blocks[0] = lax.optimization_barrier((near[0], near[1], blocks[0]))
    far = [moved(near[1][:half], x_then_y(1)), moved(near[0][half:], x_then_y(3))]
    for chunk in near:
        both = [chunk, moved(chunk, other_core)]
        blocks.append(transform(weights, scaled, both))
        pieces += both
    partial = screen(blocks, pieces)
    far[0], partial = lax.optimization_barrier((far[0], partial))
    far[1], partial = lax.optimization_barrier((far[1], partial))
    last = far + [moved(piece, other_core) for piece in far]
    return screen_last(weights, scaled, partial, last).reshape(FREQS, rows, PANEL)


def solution(mesh):
    split = Mesh(mesh.devices.reshape(SIZES), TM + PTS)
    everywhere = P(TM + PTS, None)
    placed = (P(PTS, None), everywhere, P(), P(), P(), P(), everywhere)
    return jax.shard_map(
        shards, mesh=split, in_specs=placed, out_specs=P(None, PTS + TM, None), check_vma=False
    )
```

```python
import functools
import itertools

import jax
import jax.numpy as jnp
import numpy as np
from jax import lax
from jax.experimental import pallas as pl
from jax.experimental.pallas import tpu as pltpu
from jax.sharding import Mesh
from jax.sharding import PartitionSpec as P

NOCC = 512
BANDS = 2048
PANEL = 1024
FREQS = 8
TAUS = 8
COLS = 256
STEPS = 4

TM = ("x", "ylo")
PTS = ("yhi", "z", "core")
SIZES = (4, 2, 2, 8, 2)


def moved(value, target):
    pairs = []
    for source, (x, ylo, yhi, z, core) in enumerate(itertools.product(*map(range, SIZES))):
        x, y, z, core = target(x, 2 * yhi + ylo, z, core)
        place = (x, y % 2, y // 2, z, core)
        pairs.append((source, int(np.ravel_multi_index(place, SIZES))))
    return lax.ppermute(value, TM + PTS, pairs)


def z_flip(bit):
    return lambda x, y, z, core: (x, y, z ^ bit, core)


def y_then_x(bits):
    return lambda x, y, z, core: (x ^ bits * core, y ^ bits * (1 - core), z, core)


def x_then_y(bits):
    return lambda x, y, z, core: (x ^ bits * (1 - core), y ^ bits * core, z, core)


def other_core(x, y, z, core):
    return x, y, z, 1 - core


def contract(left, right):
    return lax.dot_general(
        left, right, (((1,), (1,)), ((), ())), preferred_element_type=jnp.float32
    )


def polar_of(scaled_ref, pieces):
    occ = jnp.concatenate([p[:, :NOCC] for p in pieces], axis=0)
    vir = jnp.concatenate([p[:, NOCC:BANDS] for p in pieces], axis=0)
    return contract(scaled_ref[:, :NOCC], occ) * contract(scaled_ref[:, NOCC:], vir)


def at_frequency(weights_ref, polar, k):
    rows = polar.shape[0] // TAUS
    terms = [
        weights_ref[k * TAUS + t, :][None, :] * polar[t * rows : (t + 1) * rows] for t in range(TAUS)
    ]
    total = functools.reduce(jnp.add, terms)
    return total.astype(jnp.bfloat16)


def transform_kernel(weights_ref, scaled_ref, *refs):
    pieces, out_ref = refs[:-1], refs[-1]
    rows = scaled_ref.shape[0] // TAUS
    polar = polar_of(scaled_ref, pieces)
    for k in range(FREQS):
        out_ref[k * rows : (k + 1) * rows, :] = at_frequency(weights_ref, polar, k)


def first_kernel(weights_ref, decay_ref, rows_ref, *refs):
    pieces, (out_ref, scaled_ref) = refs[:-2], refs[-2:]
    rows = rows_ref.shape[0]
    for t in range(TAUS):
        scaled_ref[t * rows : (t + 1) * rows, :] = (
            rows_ref[...].astype(jnp.float32) * decay_ref[t, :][None, :]
        ).astype(jnp.bfloat16)
    transform_kernel(weights_ref, scaled_ref, *pieces, out_ref)


def screen_kernel(*refs):
    pieces, out_ref = refs[:-1], refs[-1]
    held = len(pieces) // 3
    blocks, pieces = pieces[:held], pieces[held:]
    coulomb = jnp.concatenate([p[:, BANDS:] for p in pieces], axis=0)
    step = out_ref.shape[0] // STEPS
    for start in range(0, out_ref.shape[0], step):
        here = slice(start, start + step)
        transformed = jnp.concatenate([b[here, :] for b in blocks], axis=1)
        out_ref[here, :] = jnp.dot(transformed, coulomb, preferred_element_type=jnp.float32)


def last_kernel(weights_ref, scaled_ref, partial_ref, *refs):
    pieces, (out_ref, done_ref, sems) = refs[:-3], refs[-3:]
    rows = scaled_ref.shape[0] // TAUS
    polar = polar_of(scaled_ref, pieces)
    coulomb = jnp.concatenate([p[:, BANDS:] for p in pieces], axis=0)
    count = FREQS // STEPS
    copies = []
    for step in range(STEPS):
        here = slice(step * count * rows, (step + 1) * count * rows)
        some = range(step * count, (step + 1) * count)
        transformed = jnp.concatenate([at_frequency(weights_ref, polar, k) for k in some], axis=0)
        product = jnp.dot(transformed, coulomb, preferred_element_type=jnp.float32)
        done_ref[here, :] = (partial_ref[here, :] + product).astype(jnp.bfloat16)
        copies.append(
            pltpu.make_async_copy(done_ref.at[here, :], out_ref.at[here, :], sems.at[step])
        )
        copies[-1].start()
    for copy in copies:
        copy.wait()


VMEM = pl.BlockSpec(memory_space=pltpu.VMEM)


def transform(weights, scaled, pieces):
    rows, width = scaled.shape[0], sum(p.shape[0] for p in pieces)
    return pl.pallas_call(
        transform_kernel,
        out_shape=jax.ShapeDtypeStruct((rows, width), jnp.bfloat16),
        in_specs=[VMEM] * (2 + len(pieces)),
        out_specs=VMEM,
        compiler_params=pltpu.CompilerParams(vmem_limit_bytes=12 * 2**20),
        cost_estimate=pl.CostEstimate(
            flops=2 * rows * width * BANDS, bytes_accessed=2**20, transcendentals=0
        ),
    )(weights, scaled, *pieces)


def transform_first(weights, decay, own, pieces):
    rows, width = TAUS * own.shape[0], sum(p.shape[0] for p in pieces)
    return pl.pallas_call(
        first_kernel,
        out_shape=[
            jax.ShapeDtypeStruct((rows, width), jnp.bfloat16),
            jax.ShapeDtypeStruct((rows, BANDS), jnp.bfloat16),
        ],
        in_specs=[VMEM] * (3 + len(pieces)),
        out_specs=[VMEM, VMEM],
        compiler_params=pltpu.CompilerParams(vmem_limit_bytes=12 * 2**20),
        cost_estimate=pl.CostEstimate(
            flops=2 * rows * width * BANDS, bytes_accessed=2**20, transcendentals=0
        ),
    )(weights, decay, own, *pieces)


def screen(blocks, pieces):
    rows = blocks[0].shape[0]
    return pl.pallas_call(
        screen_kernel,
        out_shape=jax.ShapeDtypeStruct((rows, PANEL), jnp.float32),
        in_specs=[VMEM] * (len(blocks) + len(pieces)),
        out_specs=VMEM,
        compiler_params=pltpu.CompilerParams(vmem_limit_bytes=12 * 2**20),
        cost_estimate=pl.CostEstimate(
            flops=2 * rows * COLS * len(blocks) * PANEL, bytes_accessed=2**20, transcendentals=0
        ),
    )(*blocks, *pieces)


def screen_last(weights, scaled, partial, pieces):
    rows = scaled.shape[0]
    return pl.pallas_call(
        last_kernel,
        out_shape=jax.ShapeDtypeStruct((rows, PANEL), jnp.bfloat16),
        in_specs=[VMEM] * (3 + len(pieces)),
        out_specs=pl.BlockSpec(memory_space=pl.ANY),
        scratch_shapes=[
            pltpu.VMEM((rows, PANEL), jnp.bfloat16),
            pltpu.SemaphoreType.DMA((STEPS,)),
        ],
        compiler_params=pltpu.CompilerParams(vmem_limit_bytes=12 * 2**20),
        cost_estimate=pl.CostEstimate(
            flops=2 * rows * COLS * (PANEL + BANDS), bytes_accessed=2**22, transcendentals=0
        ),
    )(weights, scaled, partial, *pieces)


def shards(orbitals, panel_orbitals, band_gap, tau_points, quad_weight, frequencies, coulomb):
    held = jnp.pad(panel_orbitals, ((0, 0), (0, PANEL))) + jnp.pad(coulomb, ((0, 0), (BANDS, 0)))
    for group in ((1,), (6, 4, 2)):
        held = jnp.concatenate([held] + [moved(held, z_flip(bits)) for bits in group], axis=0)
    rows = orbitals.shape[0] // lax.axis_size(TM)
    own = lax.dynamic_slice_in_dim(orbitals, lax.axis_index(TM) * rows, rows)
    decay = jnp.exp(-band_gap[None, :] * tau_points[:, None])
    weights = -quad_weight[None, :] * jnp.cos(frequencies[:, None] * tau_points[None, :])
    weights = jnp.broadcast_to(weights.reshape(FREQS * TAUS, 1), (FREQS * TAUS, COLS))

    held, weights, decay, own = lax.optimization_barrier((held, weights, decay, own))
    held = jnp.concatenate([held] + [moved(held, y_then_x(bits)) for bits in (2, 1, 3)], axis=0)
    half = held.shape[0] // 2
    near = [moved(held, x_then_y(bits)) for bits in (1, 3)]
    pieces = [held, moved(held, other_core)]
    block, scaled = transform_first(weights, decay, own, pieces)
    blocks = [block]
    near[0], near[1], blocks[0] = lax.optimization_barrier((near[0], near[1], blocks[0]))
    far = [moved(near[1][:half], x_then_y(1)), moved(near[0][half:], x_then_y(3))]
    for chunk in near:
        both = [chunk, moved(chunk, other_core)]
        blocks.append(transform(weights, scaled, both))
        pieces += both
    partial = screen(blocks, pieces)
    far[0], partial = lax.optimization_barrier((far[0], partial))
    far[1], partial = lax.optimization_barrier((far[1], partial))
    last = far + [moved(piece, other_core) for piece in far]
    return screen_last(weights, scaled, partial, last).reshape(FREQS, rows, PANEL)


def solution(mesh):
    split = Mesh(mesh.devices.reshape(SIZES), TM + PTS)
    everywhere = P(TM + PTS, None)
    placed = (P(PTS, None), everywhere, P(), P(), P(), P(), everywhere)
    return jax.shard_map(
        shards, mesh=split, in_specs=placed, out_specs=P(None, PTS + TM, None), check_vma=False
    )
```
